512 devices in a mesh: space: 64 (over z_lo, x, core), tm: 8 (over y, z_hi).
Axes of the slice: x: 4, y: 4, z: 16 (z_hi: 2, z_lo: 8; z = z_hi * 8 + z_lo), core: 2. Of those that a mesh axis runs over, the one named last changes fastest.
Arguments:
- query_key: bfloat16 [1, 65536, 64], P(None, 'space'), may hold values from -1.5 to 8
- selection: bfloat16 [1, 65536, 64], P(None, 'space'), may hold values from 0.19921875 to 1
- memory_key: bfloat16 [32, 65536, 64], P('tm', 'space'), may hold values from -1.5 to 1.5
- shrinkage: bfloat16 [32, 65536], P('tm', 'space'), may hold values from 1 to 4
- memory_value: bfloat16 [32, 65536, 512], P('tm', 'space'), may hold values from -6 to 6
- block_list: int32 [512, 6], P('space'), may hold values from 0 to 11, as said below
- block_count: int32 [512], P('space'), may hold values from 1 to 6, as said below
Outputs:
- readout: bfloat16 [1, 65536, 512], P(None, 'space')
The draws below stay inside these ranges and needn't reach their ends.
Inputs may be any that keep to these rules, and one draw needn't show every extreme that they name: `block_list`: entries of a row are distinct; rows of the first tile name no block under 2, rows of the last tile none of 10 or above. `block_count`: the first block of every tile uses all 6 listed blocks.
All inputs are finite; a program needn't handle non-finite values.
Results may differ from the reference program's by a relative error of at most 0.0061.
Values may be sent and summed in bfloat16 or wider, within the bound.
A program may use at most 128 MiB of HBM per device.

```python
import math
import jax
import jax.numpy as jnp
from jax import lax

CK = 64
CV = 512
BS = 128
W = 2
NL = 6
FD = 4
Q = 1
NBLK = 8
NPIX = 65536
QBLK = 512
MEM = 32
WIN = 12
N_SPACE = 64
N_TM = 8


def draw_query_key(key, part):
    base_part = jnp.clip(0.25 * jax.random.normal(key, (Q, NPIX, CK), jnp.float32), -1.5, 1.5)
    return base_part.astype(jnp.bfloat16)


def draw_block_list(key, part):
    tile_of = (jnp.arange(QBLK, dtype=jnp.int32) // NBLK)[:, None]
    slot_of = jnp.arange(WIN, dtype=jnp.int32)[None, :]
    random_part = jax.random.randint(key, (QBLK, WIN), 0, 2 ** 20)
    scores = random_part * WIN + slot_of
    barred = (tile_of == 0) & (slot_of < W) | (tile_of == N_SPACE - 1) & (slot_of >= W + NBLK)
    scores = scores + jnp.where(barred, 2 ** 28, 0)
    ignored, chosen = lax.top_k(-scores, NL)
    return chosen.astype(jnp.int32)


def draw_block_count(key, part):
    counts = jax.random.randint(key, (QBLK,), 1, NL + 1)
    leading = jnp.arange(QBLK, dtype=jnp.int32) % NBLK == 0
    return jnp.where(leading, NL, counts).astype(jnp.int32)


def shard_levels(own_key, dims, shards, low, high):
    level = 1.0
    for position, blocks in shards:
        draws = jax.random.uniform(jax.random.fold_in(jax.random.fold_in(own_key, 6), position), (blocks,), jnp.float32, low / len(shards), high / len(shards))
        level = level * jnp.repeat(jnp.exp(draws), dims[position] // blocks).reshape((-1,) + (1,) * (len(dims) - 1 - position))
    return level


def normal_values(key, extent, spread, bound, shards=(), kind=jnp.bfloat16):
    values = jax.random.normal(key, extent, jnp.float32) * spread
    if len(shards) > 0:
        values = shard_levels(key, extent, shards, -0.22, 0.18) * values
    return jnp.clip(values, min=-bound, max=bound).astype(kind)


def setup_inputs(seed: int = 0) -> dict:
    streams_of = jax.random.split(jax.random.key(seed), 8)
    query_key = draw_query_key(jax.random.fold_in(streams_of[7], 71), 0)
    selection = jnp.clip(0.19921875 + 0.80078125 * jax.random.uniform(streams_of[1], (Q, NPIX, CK), jnp.float32) ** shard_levels(streams_of[1], (Q, NPIX, CK), ((1, 64),), -0.2, 0.2), 0.19921875, 1.0).astype(jnp.bfloat16)
    memory_key = normal_values(streams_of[2], (MEM, NPIX, CK), 0.25, 1.5, ((0, 8), (1, 64)))
    shrinkage = jnp.clip(jnp.exp(math.log(4.0) - 1.3862944 * jax.random.uniform(streams_of[3], (MEM, NPIX), jnp.float32) ** shard_levels(streams_of[3], (MEM, NPIX), ((0, 8), (1, 64)), -0.2, 0.2)), 1.0, 4.0).astype(jnp.bfloat16)
    memory_value = normal_values(streams_of[4], (MEM, NPIX, CV), 1.0, 6.0, ((0, 8), (1, 64)))
    block_list = draw_block_list(jax.random.fold_in(streams_of[7], 71), 0)
    block_count = draw_block_count(jax.random.fold_in(streams_of[7], 71), 0)
    return {"query_key": query_key, "selection": selection, "memory_key": memory_key, "shrinkage": shrinkage, "memory_value": memory_value, "block_list": block_list, "block_count": block_count}


def reference(query_key, selection, memory_key, shrinkage, memory_value, block_list, block_count):
    score_scale = 1.0 / math.sqrt(CK)
    query_f = query_key.astype(jnp.float32)
    select_f = selection.astype(jnp.float32)
    query_sel = lax.optimization_barrier((2.0 * query_f * select_f).astype(jnp.bfloat16))
    self_term = lax.optimization_barrier(jnp.sum(select_f * query_f * query_f, axis=-1))
    key_square = lax.optimization_barrier((memory_key.astype(jnp.float32) ** 2).astype(jnp.bfloat16))
    key_blocks = memory_key.reshape(MEM, QBLK, BS, CK)
    square_blocks = key_square.reshape(MEM, QBLK, BS, CK)
    value_blocks = memory_value.reshape(MEM, QBLK, BS, CV)
    shrink_blocks = shrinkage.reshape(MEM, QBLK, BS)
    query_rows = query_sel.reshape(Q, QBLK, BS, CK).transpose(1, 0, 2, 3)
    select_rows = selection.reshape(Q, QBLK, BS, CK).transpose(1, 0, 2, 3)
    self_rows = self_term.reshape(Q, QBLK, BS).transpose(1, 0, 2)
    block_ids = jnp.arange(QBLK, dtype=jnp.int32)

    def one_block(inputs):
        block_id, query_blk, select_blk, self_blk, listed, live_count = inputs
        global_ids = (block_id // NBLK * NBLK + listed - W).astype(jnp.int32)
        squares = jnp.take(square_blocks, global_ids, axis=1).astype(jnp.float32)
        key_rows = jnp.take(key_blocks, global_ids, axis=1).astype(jnp.float32)
        shrink = jnp.take(shrink_blocks, global_ids, axis=1).astype(jnp.float32)
        values = jnp.take(value_blocks, global_ids, axis=1).astype(jnp.float32)
        quad_term = jnp.einsum('qrc,mjnc->qrmjn', select_blk.astype(jnp.float32), squares)
        cross_term = jnp.einsum('qrc,mjnc->qrmjn', query_blk.astype(jnp.float32), key_rows)
        scores = -shrink[None, None] * (quad_term - cross_term + self_blk[:, :, None, None, None]) * score_scale
        scores = scores.reshape(Q, BS, N_TM, FD, NL, BS)
        usable = (jnp.arange(NL, dtype=jnp.int32) < live_count)[None, None, None, None, :, None]
        group_top = lax.optimization_barrier(jnp.max(jnp.where(usable, scores, -jnp.inf), axis=(3, 4, 5)))
        shifted = scores - group_top[:, :, :, None, None, None]
        weights = jnp.where(usable, jnp.exp(shifted), jnp.zeros_like(scores))
        group_total = lax.optimization_barrier(jnp.sum(weights, axis=(3, 4, 5)))
        rounded = lax.optimization_barrier(weights.astype(jnp.bfloat16)).astype(jnp.float32)
        grouped_values = values.reshape(N_TM, FD, NL, BS, CV)
        group_sum = jnp.einsum('qrgfjn,gfjnv->qrgv', rounded, grouped_values)
        row_top = lax.optimization_barrier(jnp.max(group_top, axis=2, keepdims=True))
        factor = jnp.exp(group_top - row_top)
        summed = lax.optimization_barrier(jnp.sum(factor[:, :, :, None] * group_sum, axis=2))
        row_total = lax.optimization_barrier(jnp.sum(factor * group_total, axis=2))
        return (summed / row_total[:, :, None]).astype(jnp.bfloat16)
    blocks = lax.map(one_block, (block_ids, query_rows, select_rows, self_rows, block_list, block_count))
    return blocks.transpose(1, 0, 2, 3).reshape(Q, NPIX, CV)
```

```python
import functools
import math

import jax
import jax.numpy as jnp
from jax import lax
from jax.experimental import pallas as pl
from jax.experimental.pallas import tpu as pltpu
from jax.sharding import PartitionSpec as P

BS = 128
W = 2
NY = 4
NZ = 2
HALVES = 2
LAG_Z = 6
NEG = -1e30
MESH = pl.DeviceIdType.MESH


def kernel(
    n_space, list_ref, count_ref, query_ref, select_ref, shrink_ref, key_hbm, value_hbm, out_ref,
    key_raw, key_cat, shrink_win, value_lo, value_hi, weights, scores, tops, scales,
    lse_own, lse_all, part, part_in, zsum, zin,
    own_sem, halo_send, halo_recv, lse_send, lse_recv, y_send, y_recv, z_send, z_recv, g_send, g_recv,
):
    frames, n_blocks = key_hbm.shape[0], key_hbm.shape[1]
    n_listed = list_ref.shape[1]
    ck = key_hbm.shape[3]
    cols = value_hbm.shape[3] // HALVES
    pieces = HALVES * n_blocks
    group = frames * BS
    n_tm = NY * NZ
    scale = 1.0 / math.sqrt(ck)

    s = lax.axis_index("space")
    t = lax.axis_index("tm")
    y, zh = t // NZ, lax.rem(t, NZ)
    has_up, has_down = s < n_space - 1, s > 0
    values = (value_lo, value_hi)

    own = [pltpu.make_async_copy(key_hbm, key_raw.at[:, pl.ds(W, n_blocks)], own_sem.at[0])]
    for h in range(HALVES):
        own.append(
            pltpu.make_async_copy(
                value_hbm.at[:, :, :, pl.ds(h * cols, cols)],
                values[h].at[:, pl.ds(W, n_blocks)],
                own_sem.at[1 + h],
            )
        )
    for copy in own:
        copy.start()
    for b in range(n_blocks):
        shrink_win[W + b, 0:frames, :] = shrink_ref[:, b * BS : (b + 1) * BS].astype(jnp.float32) * (-scale)

    @pl.when(jnp.logical_not(has_down))
    def _():
        key_raw[:, 0:W] = jnp.zeros_like(key_raw[:, 0:W])
        shrink_win[0:W] = jnp.zeros_like(shrink_win[0:W])
        for v in values:
            v[:, 0:W] = jnp.zeros_like(v[:, 0:W])

    @pl.when(jnp.logical_not(has_up))
    def _():
        key_raw[:, W + n_blocks :] = jnp.zeros_like(key_raw[:, W + n_blocks :])
        shrink_win[W + n_blocks :] = jnp.zeros_like(shrink_win[W + n_blocks :])
        for v in values:
            v[:, W + n_blocks :] = jnp.zeros_like(v[:, W + n_blocks :])

    barrier = pltpu.get_barrier_semaphore()

    def peer(k):
        return (s, lax.rem(t + k, n_tm))

    def y_peer(k):
        return (s, lax.rem(y + k, NY) * NZ + zh)

    z_peer = (s, y * NZ + (1 - zh))
    for k in range(1, n_tm):
        pl.semaphore_signal(barrier, inc=1, device_id=peer(k), device_id_type=MESH)

    @pl.when(has_up)
    def _():
        pl.semaphore_signal(barrier, inc=1, device_id=(s + 1, t), device_id_type=MESH)

    @pl.when(has_down)
    def _():
        pl.semaphore_signal(barrier, inc=1, device_id=(s - 1, t), device_id_type=MESH)

    @pl.when(jnp.logical_and(has_up, has_down))
    def _():
        pl.semaphore_wait(barrier, n_tm + 1)

    @pl.when(jnp.logical_not(jnp.logical_and(has_up, has_down)))
    def _():
        pl.semaphore_wait(barrier, n_tm)

    def remote(src, dst, send, recv, to):
        return pltpu.make_async_remote_copy(
            src_ref=src, dst_ref=dst, send_sem=send, recv_sem=recv, device_id=to, device_id_type=MESH
        )

    top_blocks, low_blocks = pl.ds(n_blocks - W, W), pl.ds(0, W)
    ups, downs = [], []
    for halo, (blocks, dst_at, to) in (
        (ups, (top_blocks, pl.ds(0, W), (s + 1, t))),
        (downs, (low_blocks, pl.ds(W + n_blocks, W), (s - 1, t))),
    ):
        d = 0 if halo is ups else 1
        own_at = pl.ds(n_blocks, W) if halo is ups else pl.ds(W, W)
        halo.append(remote(key_hbm.at[:, blocks], key_raw.at[:, dst_at], halo_send.at[d, 0], halo_recv.at[d, 0], to))
        halo.append(remote(shrink_win.at[own_at], shrink_win.at[dst_at], halo_send.at[d, 1], halo_recv.at[d, 1], to))
        for h in range(HALVES):
            halo.append(
                remote(
                    value_hbm.at[:, blocks, :, pl.ds(h * cols, cols)],
                    values[h].at[:, dst_at],
                    halo_send.at[d, 2 + h],
                    halo_recv.at[d, 2 + h],
                    to,
                )
            )

    @pl.when(has_up)
    def _():
        for copy in ups:
            copy.start()

    @pl.when(has_down)
    def _():
        for copy in downs:
            copy.start()

    def halo_arrived(n):
        @pl.when(has_down)
        def _():
            ups[n].wait_recv()

        @pl.when(has_up)
        def _():
            downs[n].wait_recv()

    def widen(at):
        k = key_raw[:, at]
        kf = k.astype(jnp.float32)
        key_cat[:, at] = jnp.concatenate([(kf * kf).astype(jnp.bfloat16), k], axis=-1)

    own[0].wait()

    @pl.loop(0, n_blocks)
    def _(b):
        widen(W + b)

    halo_arrived(0)
    halo_arrived(1)
    for w in (0, 1, W + n_blocks, W + n_blocks + 1):
        widen(w)

    def lse_copy(k, b):
        return remote(lse_own.at[b], lse_all.at[t, b], lse_send.at[k, b], lse_recv.at[k, b], peer(k))

    @pl.loop(0, n_blocks)
    def _(b):
        rows = pl.ds(pl.multiple_of(b * BS, BS), BS)
        q = query_ref[0, rows, :].astype(jnp.float32)
        sel = select_ref[0, rows, :]
        sel_f = sel.astype(jnp.float32)
        self_term = jnp.sum(sel_f * q * q, axis=1, keepdims=True)
        lhs = jnp.concatenate([sel, -((2.0 * q * sel_f).astype(jnp.bfloat16))], axis=1)
        live = jnp.full((1, group), count_ref[b], jnp.int32)
        best = jnp.full((BS, BS), NEG, jnp.float32)
        for j in range(n_listed):
            w = list_ref[b, j]
            rhs = jnp.concatenate([key_cat[f, w] for f in range(frames)], axis=0)
            near = shrink_win[w]
            factor = jnp.concatenate([near[f : f + 1] for f in range(frames)], axis=1)
            dots = lax.dot_general(lhs, rhs, (((1,), (1,)), ((), ())), preferred_element_type=jnp.float32)
            score = jnp.where(live > j, (dots + self_term) * factor, NEG)
            scores[j] = score
            for f in range(frames):
                best = jnp.maximum(best, score[:, f * BS : (f + 1) * BS])
        top = jnp.max(best, axis=1, keepdims=True)
        total = jnp.zeros((BS, BS), jnp.float32)
        for j in range(n_listed):
            p = jnp.exp(scores[j] - top)
            weights[b, :, j * group : (j + 1) * group] = p.astype(jnp.bfloat16)
            for f in range(frames):
                total = total + p[:, f * BS : (f + 1) * BS]
        lse = top + jnp.log(jnp.sum(total, axis=1, keepdims=True))
        tops[b] = jnp.broadcast_to(top, (BS, BS))
        row = jnp.broadcast_to(lse, (BS, BS)).T[0:1, :]
        lse_own[b] = row
        lse_all[t, b] = row
        for k in range(1, n_tm):
            lse_copy(k, b).start()

    def lse_arrival(k, b):
        at = lse_all.at[lax.rem(t + n_tm - k, n_tm), b]
        return remote(lse_own.at[b], at, lse_send.at[k, b], lse_recv.at[k, b], peer(k))

    def y_copy(k, i):
        return remote(part.at[i, lax.rem(y + k, NY)], part_in.at[k - 1, i], y_send.at[k - 1, i], y_recv.at[k - 1, i], y_peer(k))

    def z_copy(i):
        return remote(zsum.at[i], zin.at[i], z_send.at[i], z_recv.at[i], z_peer)

    def g_copy(k, i):
        return remote(out_ref.at[i, y], out_ref.at[i, y], g_send.at[k - 1, i], g_recv.at[k - 1, i], y_peer(k))

    def g_arrival(k, i):
        at = out_ref.at[i, lax.rem(y + NY - k, NY)]
        return remote(out_ref.at[i, y], at, g_send.at[k - 1, i], g_recv.at[k - 1, i], y_peer(k))

    def stage_value(h, b):
        i = h * n_blocks + b
        acc = jnp.zeros((BS, cols), jnp.float32)
        for j in range(n_listed):
            w = list_ref[b, j]
            rhs = jnp.concatenate([values[h][f, w] for f in range(frames)], axis=0)
            acc = acc + jnp.dot(
                weights[b, :, j * group : (j + 1) * group], rhs, preferred_element_type=jnp.float32
            )
        if h == 0:
            for k in range(1, n_tm):
                lse_arrival(k, b).wait_recv()
            ls = lse_all[:, b]
            peak = jnp.max(ls, axis=0)
            whole = peak + jnp.log(jnp.sum(jnp.exp(ls - peak[None]), axis=0))
            scales[b] = jnp.exp(tops[b] - jnp.broadcast_to(whole, (BS, BS)).T)
        factor = jnp.concatenate([scales[b]] * (cols // BS), axis=1)
        part[i] = (acc * factor).astype(jnp.bfloat16).reshape(NY, BS // NY, cols)
        for k in range(1, NY):
            y_copy(k, i).start()

    def stage_y(i):
        total = part[i, y].astype(jnp.float32)
        for k in range(1, NY):
            y_copy(k, i).wait_recv()
            total = total + part_in[k - 1, i].astype(jnp.float32)
        zsum[i] = total.astype(jnp.bfloat16)
        z_copy(i).start()

    def stage_z(i):
        z_copy(i).wait_recv()
        out_ref[i, y] = (zsum[i].astype(jnp.float32) + zin[i].astype(jnp.float32)).astype(jnp.bfloat16)
        for k in range(1, NY):
            g_copy(k, i).start()

    for h in range(HALVES):
        own[1 + h].wait()
        halo_arrived(2 + h)

        @pl.loop(0, n_blocks)
        def _(b):
            i = h * n_blocks + b
            stage_value(h, b)

            @pl.when(i >= 1)
            def _():
                stage_y(i - 1)

            @pl.when(i >= LAG_Z)
            def _():
                stage_z(i - LAG_Z)

    stage_y(pieces - 1)

    @pl.loop(pieces - LAG_Z, pieces)
    def _(i):
        stage_z(i)

    @pl.loop(0, pieces)
    def _(i):
        for k in range(1, NY):
            g_arrival(k, i).wait_recv()
            y_copy(k, i).wait_send()
            g_copy(k, i).wait_send()
        z_copy(i).wait_send()

    @pl.loop(0, n_blocks)
    def _(b):
        for k in range(1, n_tm):
            lse_copy(k, b).wait_send()

    @pl.when(has_up)
    def _():
        for copy in ups:
            copy.wait_send()

    @pl.when(has_down)
    def _():
        for copy in downs:
            copy.wait_send()


def shards(n_space, query_key, selection, memory_key, shrinkage, memory_value, block_list, block_count):
    frames, pixels, ck = memory_key.shape
    cv = memory_value.shape[2]
    n_blocks = pixels // BS
    n_listed = block_list.shape[1]
    window = n_blocks + 2 * W
    cols = cv // HALVES
    pieces = HALVES * n_blocks
    n_tm = NY * NZ
    part_rows = BS // NY
    bf, f32 = jnp.bfloat16, jnp.float32
    keys = memory_key.reshape(frames, n_blocks, BS, ck)
    vals = memory_value.reshape(frames, n_blocks, BS, cv)
    vmem = pl.BlockSpec(memory_space=pltpu.VMEM)
    smem = pl.BlockSpec(memory_space=pltpu.SMEM)
    hbm = pl.BlockSpec(memory_space=pltpu.HBM)
    dma = pltpu.SemaphoreType.DMA
    out = pl.pallas_call(
        functools.partial(kernel, n_space),
        out_shape=jax.ShapeDtypeStruct((pieces, NY, part_rows, cols), bf),
        in_specs=[smem, smem, vmem, vmem, vmem, hbm, hbm],
        out_specs=vmem,
        scratch_shapes=[
            pltpu.VMEM((frames, window, BS, ck), bf),
            pltpu.VMEM((frames, window, BS, 2 * ck), bf),
            pltpu.VMEM((window, 8, BS), f32),
            pltpu.VMEM((frames, window, BS, cols), bf),
            pltpu.VMEM((frames, window, BS, cols), bf),
            pltpu.VMEM((n_blocks, BS, n_listed * frames * BS), bf),
            pltpu.VMEM((n_listed, BS, frames * BS), f32),
            pltpu.VMEM((n_blocks, BS, BS), f32),
            pltpu.VMEM((n_blocks, BS, BS), f32),
            pltpu.VMEM((n_blocks, 1, BS), f32),
            pltpu.VMEM((n_tm, n_blocks, 1, BS), f32),
            pltpu.VMEM((pieces, NY, part_rows, cols), bf),
            pltpu.VMEM((NY - 1, pieces, part_rows, cols), bf),
            pltpu.VMEM((pieces, part_rows, cols), bf),
            pltpu.VMEM((pieces, part_rows, cols), bf),
            dma((1 + HALVES,)),
            dma((2, 2 + HALVES)),
            dma((2, 2 + HALVES)),
            dma((n_tm, n_blocks)),
            dma((n_tm, n_blocks)),
            dma((NY - 1, pieces)),
            dma((NY - 1, pieces)),
            dma((pieces,)),
            dma((pieces,)),
            dma((NY - 1, pieces)),
            dma((NY - 1, pieces)),
        ],
        compiler_params=pltpu.CompilerParams(
            collective_id=0, has_side_effects=True, vmem_limit_bytes=48 << 20
        ),
    )(block_list, block_count, query_key, selection, shrinkage, keys, vals)
    out = out.reshape(HALVES, pixels, cols).transpose(1, 0, 2)
    return out.reshape(1, pixels, cv)


def solution(mesh):
    in_specs = (
        P(None, "space", None),
        P(None, "space", None),
        P("tm", "space", None),
        P("tm", "space"),
        P("tm", "space", None),
        P("space", None),
        P("space"),
    )
    out_specs = P(None, "space", None)
    return jax.shard_map(
        functools.partial(shards, mesh.shape["space"]),
        mesh=mesh,
        in_specs=in_specs,
        out_specs=out_specs,
        check_vma=False,
    )
```

```python
import functools
import math

import jax
import jax.numpy as jnp
from jax import lax
from jax.experimental import pallas as pl
from jax.experimental.pallas import tpu as pltpu
from jax.sharding import PartitionSpec as P

BS = 128
W = 2
NY = 4
NZ = 2
HALVES = 2
LAG_Y = 6
LAG_Z = 7
N_COPIES = 4
NEG = -1e30
MESH = pl.DeviceIdType.MESH


def kernel(
    n_space, list_ref, count_ref, query_hbm, select_hbm, shrink_ref, key_hbm, value_hbm, out_ref,
    query_ref, select_ref, lhs_all, self_all, key_raw, key_cat, shrink_win, value_lo, value_hi, weights, scores, inverse,
    lse_y, lse_z, turned, share_y, share_z, part, part_in, zsum, zin,
    own_sem, halo_send, halo_recv, ly_send, ly_recv, lz_send, lz_recv, y_send, y_recv, z_send, z_recv, g_send, g_recv,
):
    frames, ck = key_hbm.shape[0], key_hbm.shape[1]
    n_blocks, n_listed = list_ref.shape
    n_own, n_halo = n_blocks * BS, W * BS
    cols = value_hbm.shape[3] // HALVES
    pieces = HALVES * n_blocks
    group = frames * BS
    rows_y = BS // NY
    scale = math.log2(math.e) / math.sqrt(ck)

    s = lax.axis_index("space")
    t = lax.axis_index("tm")
    y, zh = t // NZ, lax.rem(t, NZ)
    has_up, has_down = s < n_space - 1, s > 0
    values = (value_lo, value_hi)

    own = [pltpu.make_async_copy(key_hbm, key_raw.at[:, :, pl.ds(n_halo, n_own)], own_sem.at[0])]
    for h in range(HALVES):
        own.append(
            pltpu.make_async_copy(
                value_hbm.at[:, :, :, pl.ds(h * cols, cols)],
                values[h].at[:, pl.ds(W, n_blocks)],
                own_sem.at[1 + h],
            )
        )
    own[0].start()
    queries = [
        pltpu.make_async_copy(query_hbm, query_ref, own_sem.at[1 + HALVES]),
        pltpu.make_async_copy(select_hbm, select_ref, own_sem.at[2 + HALVES]),
    ]
    for copy in queries:
        copy.start()
    def shrink_own(b):
        near = shrink_ref[:, b * BS : (b + 1) * BS].astype(jnp.float32) * (-scale)
        shrink_win[W + b] = jnp.concatenate([near[f : f + 1] for f in range(frames)], axis=1)

    for b in range(n_blocks):
        shrink_own(b)

    @pl.when(jnp.logical_not(has_down))
    def _():
        key_raw[:, :, 0:n_halo] = jnp.zeros((frames, ck, n_halo), key_raw.dtype)
        shrink_win[0:W] = jnp.zeros_like(shrink_win[0:W])
        for v in values:
            v[:, 0:W] = jnp.zeros_like(v[:, 0:W])

    @pl.when(jnp.logical_not(has_up))
    def _():
        key_raw[:, :, n_halo + n_own :] = jnp.zeros((frames, ck, n_halo), key_raw.dtype)
        shrink_win[W + n_blocks :] = jnp.zeros_like(shrink_win[W + n_blocks :])
        for v in values:
            v[:, W + n_blocks :] = jnp.zeros_like(v[:, W + n_blocks :])

    barrier = pltpu.get_barrier_semaphore()

    def y_peer(k):
        return (s, lax.rem(y + k, NY) * NZ + zh)

    z_peer = (s, y * NZ + (1 - zh))
    for to in (y_peer(1), y_peer(2), y_peer(3), z_peer):
        pl.semaphore_signal(barrier, inc=1, device_id=to, device_id_type=MESH)

    @pl.when(has_up)
    def _():
        pl.semaphore_signal(barrier, inc=1, device_id=(s + 1, t), device_id_type=MESH)

    @pl.when(has_down)
    def _():
        pl.semaphore_signal(barrier, inc=1, device_id=(s - 1, t), device_id_type=MESH)

    def widen(w):
        at = pl.ds(pl.multiple_of(w * BS, BS), BS)
        for f in range(frames):
            k = key_raw[f, :, at]
            kf = k.astype(jnp.float32)
            key_cat[w, 0:ck, f * BS : (f + 1) * BS] = (kf * kf).astype(jnp.bfloat16)
            key_cat[w, ck : 2 * ck, f * BS : (f + 1) * BS] = k

    own[0].wait()

    @pl.loop(0, n_blocks)
    def _(b):
        widen(W + b)

    pl.semaphore_wait(barrier, NY + has_up.astype(jnp.int32) + has_down.astype(jnp.int32))

    def remote(src, dst, send, recv, to):
        return pltpu.make_async_remote_copy(
            src_ref=src, dst_ref=dst, send_sem=send, recv_sem=recv, device_id=to, device_id_type=MESH
        )

    top_blocks, low_blocks = pl.ds(n_blocks - W, W), pl.ds(0, W)
    ups, downs = [], []
    for halo, (blocks, dst_at, to) in (
        (ups, (top_blocks, pl.ds(0, W), (s + 1, t))),
        (downs, (low_blocks, pl.ds(W + n_blocks, W), (s - 1, t))),
    ):
        d = 0 if halo is ups else 1
        own_at = pl.ds(n_blocks, W) if halo is ups else pl.ds(W, W)
        key_from = pl.ds(n_own - n_halo, n_halo) if halo is ups else pl.ds(0, n_halo)
        key_to = pl.ds(0, n_halo) if halo is ups else pl.ds(n_halo + n_own, n_halo)
        halo.append(
            remote(
                key_hbm.at[:, :, key_from], key_raw.at[:, :, key_to], halo_send.at[d, 0], halo_recv.at[d, 0], to
            )
        )
        halo.append(remote(shrink_win.at[own_at], shrink_win.at[dst_at], halo_send.at[d, 1], halo_recv.at[d, 1], to))
        for h in range(HALVES):
            halo.append(
                remote(
                    value_hbm.at[:, blocks, :, pl.ds(h * cols, cols)],
                    values[h].at[:, dst_at],
                    halo_send.at[d, 2 + h],
                    halo_recv.at[d, 2 + h],
                    to,
                )
            )

    @pl.when(has_up)
    def _():
        for copy in ups:
            copy.start()

    @pl.when(has_down)
    def _():
        for copy in downs:
            copy.start()

    def halo_arrived(n):
        @pl.when(has_down)
        def _():
            ups[n].wait_recv()

        @pl.when(has_up)
        def _():
            downs[n].wait_recv()

    for copy in own[1:]:
        copy.start()
    for copy in queries:
        copy.wait()

    @pl.loop(0, n_blocks)
    def _(b):
        at = pl.ds(pl.multiple_of(b * BS, BS), BS)
        sel = select_ref[0, :, at].astype(jnp.float32)
        q = query_ref[0, :, at].astype(jnp.float32)
        lhs = jnp.concatenate([sel, -2.0 * q * sel], axis=0).T.astype(jnp.bfloat16)
        self_term = jnp.broadcast_to(jnp.sum(sel * q * q, axis=0, keepdims=True), (BS, BS)).T
        lhs_all[b] = lhs
        self_all[b] = self_term

    halo_arrived(0)
    halo_arrived(1)
    for w in (0, 1, W + n_blocks, W + n_blocks + 1):
        widen(w)

    @pl.loop(0, n_blocks)
    def _(b):
        self_term = jnp.concatenate([self_all[b]] * frames, axis=1)
        live = jnp.full((1, BS), count_ref[b], jnp.int32)
        best = jnp.full((BS, BS), NEG, jnp.float32)
        for j in range(n_listed):
            w = list_ref[b, j]
            dots = jnp.dot(lhs_all[b], key_cat[w], preferred_element_type=jnp.float32)
            score = (dots + self_term) * shrink_win[w]
            scores[j] = score
            most = score[:, 0:BS]
            for f in range(1, frames):
                most = jnp.maximum(most, score[:, f * BS : (f + 1) * BS])
            best = jnp.maximum(best, jnp.where(live > j, most, NEG))
        top = jnp.max(best, axis=1, keepdims=True)
        total = jnp.zeros((BS, BS), jnp.float32)
        for j in range(n_listed):
            under = jnp.where(live > j, jnp.broadcast_to(top, (BS, BS)), -NEG)
            for f in range(frames):
                p = jnp.exp2(scores[j, :, f * BS : (f + 1) * BS] - under)
                weights[b, :, (j * frames + f) * BS : (j * frames + f + 1) * BS] = p.astype(jnp.bfloat16)
                total = total + p
        whole = jnp.sum(total, axis=1, keepdims=True)
        inverse[b] = jnp.broadcast_to(1.0 / whole, (BS, BS))
        lse_y[0, b] = jnp.broadcast_to(top + jnp.log2(whole), (BS, BS)).T[0:1, :]

    def ly_copy(k):
        return remote(lse_y.at[0], lse_y.at[k], ly_send.at[k - 1], ly_recv.at[k - 1], y_peer(k))

    lz_copy = remote(lse_z.at[0], lse_z.at[1], lz_send.at[0], lz_recv.at[0], z_peer)
    for k in range(1, NY):
        ly_copy(k).start()

    def spread(levels, share):
        peak = functools.reduce(jnp.maximum, levels)
        whole = peak + jnp.log2(functools.reduce(jnp.add, [jnp.exp2(level - peak) for level in levels]))
        factors = jnp.concatenate([jnp.exp2(level - whole) for level in levels], axis=0)
        rest = jnp.zeros((BS - factors.shape[0], BS), jnp.float32)
        turned[...] = jnp.concatenate([factors, rest], axis=0).T
        mine = turned[pl.ds(pl.multiple_of(y * rows_y, rows_y), rows_y), :]
        for g in range(len(levels)):
            for b in range(n_blocks):
                n = g * n_blocks + b
                share[g, b] = jnp.broadcast_to(mine[:, n : n + 1], (rows_y, BS))
        return whole

    def level(ref, g):
        return jnp.concatenate([ref[g, b] for b in range(n_blocks)], axis=0)

    def wide(x):
        return jnp.concatenate([x] * (cols // BS), axis=1)

    def y_copy(k, i):
        return remote(part.at[i, lax.rem(y + k, NY)], part_in.at[k - 1, i], y_send.at[k - 1, i], y_recv.at[k - 1, i], y_peer(k))

    def z_copy(i):
        return remote(zsum.at[i], zin.at[i], z_send.at[i], z_recv.at[i], z_peer)

    def out_at(i, yy):
        at = pl.ds(pl.multiple_of(lax.div(i, n_blocks) * cols, cols), cols)
        return out_ref.at[lax.rem(i, n_blocks), yy, :, at]

    def g_copy(k, i):
        return remote(out_at(i, y), out_at(i, y), g_send.at[k - 1, i], g_recv.at[k - 1, i], y_peer(k))

    def g_arrival(k, i):
        at = out_at(i, lax.rem(y + NY - k, NY))
        return remote(out_at(i, y), at, g_send.at[k - 1, i], g_recv.at[k - 1, i], y_peer(k))

    def stage_value(h, b):
        i = h * n_blocks + b
        acc = jnp.zeros((BS, cols), jnp.float32)
        for j in range(n_listed):
            w = list_ref[b, j]
            rhs = jnp.concatenate([values[h][f, w] for f in range(frames)], axis=0)
            acc = acc + jnp.dot(
                weights[b, :, j * group : (j + 1) * group], rhs, preferred_element_type=jnp.float32
            )
        part[i] = (acc * wide(inverse[b])).astype(jnp.bfloat16).reshape(NY, BS // NY, cols)
        for k in range(1, NY):
            y_copy(k, i).start()

    def stage_y(i):
        b = lax.rem(i, n_blocks)
        total = part[i, y].astype(jnp.float32) * wide(share_y[0, b])
        for k in range(1, NY):
            y_copy(k, i).wait_recv()
            total = total + part_in[k - 1, i].astype(jnp.float32) * wide(share_y[k, b])
        zsum[i] = total.astype(jnp.bfloat16)
        z_copy(i).start()

    def stage_z(i):
        b = lax.rem(i, n_blocks)
        z_copy(i).wait_recv()
        mine, other = zsum[i].astype(jnp.float32), zin[i].astype(jnp.float32)
        low, high = jnp.where(zh == 0, mine, other), jnp.where(zh == 0, other, mine)
        out_at(i, y)[...] = (low * wide(share_z[0, b]) + high * wide(share_z[1, b])).astype(jnp.bfloat16)
        for k in range(1, NY):
            g_copy(k, i).start()

    own[1].wait()
    halo_arrived(2)

    @pl.loop(0, LAG_Y)
    def _(b):
        stage_value(0, b)

    for k in range(1, NY):
        ly_copy(k).wait_recv()
    local = spread([level(lse_y, k) for k in range(NY)], share_y)
    for b in range(n_blocks):
        lse_z[0, b] = local[b : b + 1]

    lz_copy.start()

    @pl.loop(LAG_Y, n_blocks)
    def _(b):
        stage_value(0, b)
        stage_y(b - LAG_Y)

    own[2].wait()
    halo_arrived(3)

    @pl.loop(0, LAG_Z)
    def _(b):
        stage_value(1, b)
        stage_y(n_blocks + b - LAG_Y)

    lz_copy.wait_recv()
    mine, other = level(lse_z, 0), level(lse_z, 1)
    spread([jnp.where(zh == 0, mine, other), jnp.where(zh == 0, other, mine)], share_z)

    @pl.loop(LAG_Z, n_blocks)
    def _(b):
        stage_value(1, b)
        stage_y(n_blocks + b - LAG_Y)
        stage_z(b - LAG_Z)

    @pl.loop(pieces - LAG_Y, pieces)
    def _(i):
        stage_y(i)
        stage_z(i + LAG_Y - n_blocks - LAG_Z)

    @pl.loop(n_blocks + LAG_Y - LAG_Z, pieces)
    def _(i):
        stage_z(i)

    @pl.loop(0, pieces)
    def _(i):
        for k in range(1, NY):
            g_arrival(k, i).wait_recv()
            y_copy(k, i).wait_send()
            g_copy(k, i).wait_send()
        z_copy(i).wait_send()

    for k in range(1, NY):
        ly_copy(k).wait_send()
    lz_copy.wait_send()

    @pl.when(has_up)
    def _():
        for copy in ups:
            copy.wait_send()

    @pl.when(has_down)
    def _():
        for copy in downs:
            copy.wait_send()


def hand_over(x_ref, out_ref, held, in_sem, out_sem):
    rows = x_ref.shape[1] // N_COPIES
    ins, outs = [], []
    for n in range(N_COPIES):
        at = pl.ds(n * rows, rows)
        ins.append(pltpu.make_async_copy(x_ref.at[:, at], held.at[:, at], in_sem.at[n]))
        outs.append(pltpu.make_async_copy(held.at[:, at], out_ref.at[:, at], out_sem.at[n]))
    for copy in ins:
        copy.start()
    for n in range(N_COPIES):
        ins[n].wait()
        outs[n].start()
    for copy in outs:
        copy.wait()


def shards(n_space, query_key, selection, memory_key, shrinkage, memory_value, block_list, block_count):
    frames, pixels, ck = memory_key.shape
    query_key, selection = query_key.transpose(0, 2, 1), selection.transpose(0, 2, 1)
    cv = memory_value.shape[2]
    n_blocks = pixels // BS
    n_listed = block_list.shape[1]
    window = n_blocks + 2 * W
    cols = cv // HALVES
    pieces = HALVES * n_blocks
    part_rows = BS // NY
    bf, f32 = jnp.bfloat16, jnp.float32
    keys = memory_key.transpose(0, 2, 1)
    vals = memory_value.reshape(frames, n_blocks, BS, cv)
    vmem = pl.BlockSpec(memory_space=pltpu.VMEM)
    smem = pl.BlockSpec(memory_space=pltpu.SMEM)
    hbm = pl.BlockSpec(memory_space=pltpu.HBM)
    dma = pltpu.SemaphoreType.DMA
    out = pl.pallas_call(
        functools.partial(kernel, n_space),
        out_shape=jax.ShapeDtypeStruct((n_blocks, NY, part_rows, cv), bf),
        in_specs=[smem, smem, hbm, hbm, vmem, hbm, hbm],
        out_specs=vmem,
        scratch_shapes=[
            pltpu.VMEM((1, ck, pixels), bf),
            pltpu.VMEM((1, ck, pixels), bf),
            pltpu.VMEM((n_blocks, BS, 2 * ck), bf),
            pltpu.VMEM((n_blocks, BS, BS), f32),
            pltpu.VMEM((frames, ck, window * BS), bf),
            pltpu.VMEM((window, 2 * ck, frames * BS), bf),
            pltpu.VMEM((window, 1, frames * BS), f32),
            pltpu.VMEM((frames, window, BS, cols), bf),
            pltpu.VMEM((frames, window, BS, cols), bf),
            pltpu.VMEM((n_blocks, BS, n_listed * frames * BS), bf),
            pltpu.VMEM((n_listed, BS, frames * BS), f32),
            pltpu.VMEM((n_blocks, BS, BS), f32),
            pltpu.VMEM((NY, n_blocks, 1, BS), f32),
            pltpu.VMEM((NZ, n_blocks, 1, BS), f32),
            pltpu.VMEM((BS, BS), f32),
            pltpu.VMEM((NY, n_blocks, part_rows, BS), f32),
            pltpu.VMEM((NZ, n_blocks, part_rows, BS), f32),
            pltpu.VMEM((pieces, NY, part_rows, cols), bf),
            pltpu.VMEM((NY - 1, pieces, part_rows, cols), bf),
            pltpu.VMEM((pieces, part_rows, cols), bf),
            pltpu.VMEM((pieces, part_rows, cols), bf),
            dma((3 + HALVES,)),
            dma((2, 2 + HALVES)),
            dma((2, 2 + HALVES)),
            dma((NY - 1,)),
            dma((NY - 1,)),
            dma((1,)),
            dma((1,)),
            dma((NY - 1, pieces)),
            dma((NY - 1, pieces)),
            dma((pieces,)),
            dma((pieces,)),
            dma((NY - 1, pieces)),
            dma((NY - 1, pieces)),
        ],
        compiler_params=pltpu.CompilerParams(
            collective_id=0, has_side_effects=True, vmem_limit_bytes=60 << 20
        ),
    )(block_list, block_count, query_key, selection, shrinkage, keys, vals)
    return pl.pallas_call(
        hand_over,
        out_shape=jax.ShapeDtypeStruct((1, pixels, cv), bf),
        in_specs=[hbm],
        out_specs=hbm,
        scratch_shapes=[pltpu.VMEM((1, pixels, cv), bf), dma((N_COPIES,)), dma((N_COPIES,))],
    )(out.reshape(1, pixels, cv))


def solution(mesh):
    in_specs = (
        P(None, "space", None),
        P(None, "space", None),
        P("tm", "space", None),
        P("tm", "space"),
        P("tm", "space", None),
        P("space", None),
        P("space"),
    )
    out_specs = P(None, "space", None)
    return jax.shard_map(
        functools.partial(shards, mesh.shape["space"]),
        mesh=mesh,
        in_specs=in_specs,
        out_specs=out_specs,
        check_vma=False,
    )
```

```python
import functools
import math

import jax
import jax.numpy as jnp
from jax import lax
from jax.experimental import pallas as pl
from jax.experimental.pallas import tpu as pltpu
from jax.sharding import PartitionSpec as P

BS = 128
W = 2
NY = 4
NZ = 2
HALVES = 2
LAG_Y = 3
N_COPIES = 4
FAR_FIRST = (2, 1, 3)
NEG = -1e30
MESH = pl.DeviceIdType.MESH


def kernel(
    n_space, list_ref, count_ref, query_hbm, select_hbm, shrink_ref, key_hbm, value_hbm, out_ref,
    query_ref, select_ref, lhs_all, self_all, key_raw, key_cat, shrink_win, value_lo, value_hi, weights, scores, inverse,
    lse_y, lse_z, turned, share_y, share_z, part, part_in, zsum, zin,
    own_sem, halo_send, halo_recv, ly_send, ly_recv, lz_send, lz_recv, y_send, y_recv, z_send, z_recv, g_send, g_recv,
):
    frames, ck = key_hbm.shape[0], key_hbm.shape[1]
    n_blocks, n_listed = list_ref.shape
    n_own, n_halo = n_blocks * BS, W * BS
    cols = value_hbm.shape[3] // HALVES
    pieces = HALVES * n_blocks
    group = frames * BS
    rows_y = BS // NY
    scale = math.log2(math.e) / math.sqrt(ck)

    s = lax.axis_index("space")
    t = lax.axis_index("tm")
    y, zh = t // NZ, lax.rem(t, NZ)
    has_up, has_down = s < n_space - 1, s > 0
    values = (value_lo, value_hi)

    own = [pltpu.make_async_copy(key_hbm, key_raw.at[:, :, pl.ds(n_halo, n_own)], own_sem.at[0])]
    for h in range(HALVES):
        own.append(
            pltpu.make_async_copy(
                value_hbm.at[:, :, :, pl.ds(h * cols, cols)],
                values[h].at[:, pl.ds(W, n_blocks)],
                own_sem.at[1 + h],
            )
        )
    own[0].start()
    queries = [
        pltpu.make_async_copy(query_hbm, query_ref, own_sem.at[1 + HALVES]),
        pltpu.make_async_copy(select_hbm, select_ref, own_sem.at[2 + HALVES]),
    ]
    for copy in queries:
        copy.start()
    def shrink_own(b):
        near = shrink_ref[:, b * BS : (b + 1) * BS].astype(jnp.float32) * (-scale)
        shrink_win[W + b] = jnp.concatenate([near[f : f + 1] for f in range(frames)], axis=1)

    for b in range(n_blocks):
        shrink_own(b)

    @pl.when(jnp.logical_not(has_down))
    def _():
        key_raw[:, :, 0:n_halo] = jnp.zeros((frames, ck, n_halo), key_raw.dtype)
        shrink_win[0:W] = jnp.zeros_like(shrink_win[0:W])
        for v in values:
            v[:, 0:W] = jnp.zeros_like(v[:, 0:W])

    @pl.when(jnp.logical_not(has_up))
    def _():
        key_raw[:, :, n_halo + n_own :] = jnp.zeros((frames, ck, n_halo), key_raw.dtype)
        shrink_win[W + n_blocks :] = jnp.zeros_like(shrink_win[W + n_blocks :])
        for v in values:
            v[:, W + n_blocks :] = jnp.zeros_like(v[:, W + n_blocks :])

    barrier = pltpu.get_barrier_semaphore()

    def y_peer(k):
        return (s, lax.rem(y + k, NY) * NZ + zh)

    z_peer = (s, y * NZ + (1 - zh))
    for to in (y_peer(1), y_peer(2), y_peer(3), z_peer):
        pl.semaphore_signal(barrier, inc=1, device_id=to, device_id_type=MESH)

    @pl.when(has_up)
    def _():
        pl.semaphore_signal(barrier, inc=1, device_id=(s + 1, t), device_id_type=MESH)

    @pl.when(has_down)
    def _():
        pl.semaphore_signal(barrier, inc=1, device_id=(s - 1, t), device_id_type=MESH)

    def widen(w):
        at = pl.ds(pl.multiple_of(w * BS, BS), BS)
        for f in range(frames):
            k = key_raw[f, :, at]
            kf = k.astype(jnp.float32)
            key_cat[w, 0:ck, f * BS : (f + 1) * BS] = (kf * kf).astype(jnp.bfloat16)
            key_cat[w, ck : 2 * ck, f * BS : (f + 1) * BS] = k

    own[0].wait()

    @pl.loop(0, n_blocks)
    def _(b):
        widen(W + b)

    pl.semaphore_wait(barrier, NY + has_up.astype(jnp.int32) + has_down.astype(jnp.int32))

    def remote(src, dst, send, recv, to):
        return pltpu.make_async_remote_copy(
            src_ref=src, dst_ref=dst, send_sem=send, recv_sem=recv, device_id=to, device_id_type=MESH
        )

    top_blocks, low_blocks = pl.ds(n_blocks - W, W), pl.ds(0, W)
    ups, downs = [], []
    for halo, (blocks, dst_at, to) in (
        (ups, (top_blocks, pl.ds(0, W), (s + 1, t))),
        (downs, (low_blocks, pl.ds(W + n_blocks, W), (s - 1, t))),
    ):
        d = 0 if halo is ups else 1
        own_at = pl.ds(n_blocks, W) if halo is ups else pl.ds(W, W)
        key_from = pl.ds(n_own - n_halo, n_halo) if halo is ups else pl.ds(0, n_halo)
        key_to = pl.ds(0, n_halo) if halo is ups else pl.ds(n_halo + n_own, n_halo)
        halo.append(
            remote(
                key_hbm.at[:, :, key_from], key_raw.at[:, :, key_to], halo_send.at[d, 0], halo_recv.at[d, 0], to
            )
        )
        halo.append(remote(shrink_win.at[own_at], shrink_win.at[dst_at], halo_send.at[d, 1], halo_recv.at[d, 1], to))
        for h in range(HALVES):
            halo.append(
                remote(
                    value_hbm.at[:, blocks, :, pl.ds(h * cols, cols)],
                    values[h].at[:, dst_at],
                    halo_send.at[d, 2 + h],
                    halo_recv.at[d, 2 + h],
                    to,
                )
            )

    for first, last in ((0, 2), (2, 3), (3, 4)):

        @pl.when(has_up)
        def _():
            for copy in ups[first:last]:
                copy.start()

        @pl.when(has_down)
        def _():
            for copy in downs[first:last]:
                copy.start()

    def halo_arrived(n):
        @pl.when(has_down)
        def _():
            ups[n].wait_recv()

        @pl.when(has_up)
        def _():
            downs[n].wait_recv()

    for copy in own[1:]:
        copy.start()
    for copy in queries:
        copy.wait()

    @pl.loop(0, n_blocks)
    def _(b):
        at = pl.ds(pl.multiple_of(b * BS, BS), BS)
        sel = select_ref[0, :, at].astype(jnp.float32)
        q = query_ref[0, :, at].astype(jnp.float32)
        lhs = jnp.concatenate([sel, -2.0 * q * sel], axis=0).T.astype(jnp.bfloat16)
        self_term = jnp.broadcast_to(jnp.sum(sel * q * q, axis=0, keepdims=True), (BS, BS)).T
        lhs_all[b] = lhs
        self_all[b] = self_term

    halo_arrived(0)
    halo_arrived(1)
    for w in (0, 1, W + n_blocks, W + n_blocks + 1):
        widen(w)

    @pl.loop(0, n_blocks)
    def _(b):
        self_term = jnp.concatenate([self_all[b]] * frames, axis=1)
        live = jnp.full((1, BS), count_ref[b], jnp.int32)
        best = jnp.full((BS, BS), NEG, jnp.float32)
        for j in range(n_listed):
            w = list_ref[b, j]
            dots = jnp.dot(lhs_all[b], key_cat[w], preferred_element_type=jnp.float32)
            score = (dots + self_term) * shrink_win[w]
            scores[j] = score
            most = score[:, 0:BS]
            for f in range(1, frames):
                most = jnp.maximum(most, score[:, f * BS : (f + 1) * BS])
            best = jnp.maximum(best, jnp.where(live > j, most, NEG))
        top = jnp.max(best, axis=1, keepdims=True)
        total = jnp.zeros((BS, BS), jnp.float32)
        for j in range(n_listed):
            under = jnp.where(live > j, jnp.broadcast_to(top, (BS, BS)), -NEG)
            for f in range(frames):
                p = jnp.exp2(scores[j, :, f * BS : (f + 1) * BS] - under)
                weights[b, :, (j * frames + f) * BS : (j * frames + f + 1) * BS] = p.astype(jnp.bfloat16)
                total = total + p
        whole = jnp.sum(total, axis=1, keepdims=True)
        inverse[b] = jnp.broadcast_to(1.0 / whole, (BS, BS))
        lse_y[0, b] = jnp.broadcast_to(top + jnp.log2(whole), (BS, BS)).T[0:1, :]

    def ly_copy(k):
        return remote(lse_y.at[0], lse_y.at[k], ly_send.at[k - 1], ly_recv.at[k - 1], y_peer(k))

    lz_copy = remote(lse_z.at[0], lse_z.at[1], lz_send.at[0], lz_recv.at[0], z_peer)
    for k in range(1, NY):
        ly_copy(k).start()

    def spread(levels, share):
        peak = functools.reduce(jnp.maximum, levels)
        whole = peak + jnp.log2(functools.reduce(jnp.add, [jnp.exp2(level - peak) for level in levels]))
        factors = jnp.concatenate([jnp.exp2(level - whole) for level in levels], axis=0)
        rest = jnp.zeros((BS - factors.shape[0], BS), jnp.float32)
        turned[...] = jnp.concatenate([factors, rest], axis=0).T
        mine = turned[pl.ds(pl.multiple_of(y * rows_y, rows_y), rows_y), :]
        for g in range(len(levels)):
            for b in range(n_blocks):
                n = g * n_blocks + b
                share[g, b] = jnp.broadcast_to(mine[:, n : n + 1], (rows_y, BS))
        return whole

    def level(ref, g):
        return jnp.concatenate([ref[g, b] for b in range(n_blocks)], axis=0)

    def wide(x):
        return jnp.concatenate([x] * (cols // BS), axis=1)

    def y_copy(k, i):
        return remote(part.at[i, lax.rem(y + k, NY)], part_in.at[k - 1, i], y_send.at[k - 1, i], y_recv.at[k - 1, i], y_peer(k))

    def z_copy(i):
        return remote(zsum.at[i], zin.at[i], z_send.at[i], z_recv.at[i], z_peer)

    def out_at(i, yy):
        at = pl.ds(pl.multiple_of(lax.div(i, n_blocks) * cols, cols), cols)
        return out_ref.at[lax.rem(i, n_blocks), yy, :, at]

    def g_copy(k, i):
        return remote(out_at(i, y), out_at(i, y), g_send.at[k - 1, i], g_recv.at[k - 1, i], y_peer(k))

    def g_arrival(k, i):
        at = out_at(i, lax.rem(y + NY - k, NY))
        return remote(out_at(i, y), at, g_send.at[k - 1, i], g_recv.at[k - 1, i], y_peer(k))

    def stage_value(h, b):
        i = h * n_blocks + b
        acc = jnp.zeros((BS, cols), jnp.float32)
        for j in range(n_listed):
            w = list_ref[b, j]
            rhs = jnp.concatenate([values[h][f, w] for f in range(frames)], axis=0)
            acc = acc + jnp.dot(
                weights[b, :, j * group : (j + 1) * group], rhs, preferred_element_type=jnp.float32
            )
        part[i] = (acc * wide(inverse[b])).astype(jnp.bfloat16).reshape(NY, BS // NY, cols)
        for k in FAR_FIRST:
            y_copy(k, i).start()

    def stage_y(i):
        b = lax.rem(i, n_blocks)
        total = part[i, y].astype(jnp.float32) * wide(share_y[0, b])
        for k in range(1, NY):
            y_copy(k, i).wait_recv()
            total = total + part_in[k - 1, i].astype(jnp.float32) * wide(share_y[k, b])
        zsum[i] = total.astype(jnp.bfloat16)
        z_copy(i).start()

    def stage_z(i):
        b = lax.rem(i, n_blocks)
        z_copy(i).wait_recv()
        mine, other = zsum[i].astype(jnp.float32), zin[i].astype(jnp.float32)
        low, high = jnp.where(zh == 0, mine, other), jnp.where(zh == 0, other, mine)
        out_at(i, y)[...] = (low * wide(share_z[0, b]) + high * wide(share_z[1, b])).astype(jnp.bfloat16)
        for k in FAR_FIRST:
            g_copy(k, i).start()

    own[1].wait()
    halo_arrived(2)

    @pl.loop(0, LAG_Y)
    def _(b):
        stage_value(0, b)

    for k in range(1, NY):
        ly_copy(k).wait_recv()
    local = spread([level(lse_y, k) for k in range(NY)], share_y)
    for b in range(n_blocks):
        lse_z[0, b] = local[b : b + 1]

    lz_copy.start()

    @pl.loop(LAG_Y, n_blocks)
    def _(b):
        stage_value(0, b)
        stage_y(b - LAG_Y)

    own[2].wait()
    halo_arrived(3)

    @pl.loop(0, n_blocks)
    def _(b):
        stage_value(1, b)
        stage_y(n_blocks + b - LAG_Y)

    lz_copy.wait_recv()
    mine, other = level(lse_z, 0), level(lse_z, 1)
    spread([jnp.where(zh == 0, mine, other), jnp.where(zh == 0, other, mine)], share_z)

    @pl.loop(pieces - LAG_Y, pieces)
    def _(i):
        stage_y(i)
        stage_z(i + LAG_Y - pieces)

    @pl.loop(LAG_Y, pieces)
    def _(i):
        stage_z(i)

    @pl.loop(0, pieces)
    def _(i):
        for k in range(1, NY):
            g_arrival(k, i).wait_recv()
            y_copy(k, i).wait_send()
            g_copy(k, i).wait_send()
        z_copy(i).wait_send()

    for k in range(1, NY):
        ly_copy(k).wait_send()
    lz_copy.wait_send()

    @pl.when(has_up)
    def _():
        for copy in ups:
            copy.wait_send()

    @pl.when(has_down)
    def _():
        for copy in downs:
            copy.wait_send()


def hand_over(x_ref, out_ref, held, in_sem, out_sem):
    rows = x_ref.shape[1] // N_COPIES
    ins, outs = [], []
    for n in range(N_COPIES):
        at = pl.ds(n * rows, rows)
        ins.append(pltpu.make_async_copy(x_ref.at[:, at], held.at[:, at], in_sem.at[n]))
        outs.append(pltpu.make_async_copy(held.at[:, at], out_ref.at[:, at], out_sem.at[n]))
    for copy in ins:
        copy.start()
    for n in range(N_COPIES):
        ins[n].wait()
        outs[n].start()
    for copy in outs:
        copy.wait()


def shards(n_space, query_key, selection, memory_key, shrinkage, memory_value, block_list, block_count):
    frames, pixels, ck = memory_key.shape
    query_key, selection = query_key.transpose(0, 2, 1), selection.transpose(0, 2, 1)
    cv = memory_value.shape[2]
    n_blocks = pixels // BS
    n_listed = block_list.shape[1]
    window = n_blocks + 2 * W
    cols = cv // HALVES
    pieces = HALVES * n_blocks
    part_rows = BS // NY
    bf, f32 = jnp.bfloat16, jnp.float32
    keys = memory_key.transpose(0, 2, 1)
    vals = memory_value.reshape(frames, n_blocks, BS, cv)
    vmem = pl.BlockSpec(memory_space=pltpu.VMEM)
    smem = pl.BlockSpec(memory_space=pltpu.SMEM)
    hbm = pl.BlockSpec(memory_space=pltpu.HBM)
    dma = pltpu.SemaphoreType.DMA
    out = pl.pallas_call(
        functools.partial(kernel, n_space),
        out_shape=jax.ShapeDtypeStruct((n_blocks, NY, part_rows, cv), bf),
        in_specs=[smem, smem, hbm, hbm, vmem, hbm, hbm],
        out_specs=vmem,
        scratch_shapes=[
            pltpu.VMEM((1, ck, pixels), bf),
            pltpu.VMEM((1, ck, pixels), bf),
            pltpu.VMEM((n_blocks, BS, 2 * ck), bf),
            pltpu.VMEM((n_blocks, BS, BS), f32),
            pltpu.VMEM((frames, ck, window * BS), bf),
            pltpu.VMEM((window, 2 * ck, frames * BS), bf),
            pltpu.VMEM((window, 1, frames * BS), f32),
            pltpu.VMEM((frames, window, BS, cols), bf),
            pltpu.VMEM((frames, window, BS, cols), bf),
            pltpu.VMEM((n_blocks, BS, n_listed * frames * BS), bf),
            pltpu.VMEM((n_listed, BS, frames * BS), f32),
            pltpu.VMEM((n_blocks, BS, BS), f32),
            pltpu.VMEM((NY, n_blocks, 1, BS), f32),
            pltpu.VMEM((NZ, n_blocks, 1, BS), f32),
            pltpu.VMEM((BS, BS), f32),
            pltpu.VMEM((NY, n_blocks, part_rows, BS), f32),
            pltpu.VMEM((NZ, n_blocks, part_rows, BS), f32),
            pltpu.VMEM((pieces, NY, part_rows, cols), bf),
            pltpu.VMEM((NY - 1, pieces, part_rows, cols), bf),
            pltpu.VMEM((pieces, part_rows, cols), bf),
            pltpu.VMEM((pieces, part_rows, cols), bf),
            dma((3 + HALVES,)),
            dma((2, 2 + HALVES)),
            dma((2, 2 + HALVES)),
            dma((NY - 1,)),
            dma((NY - 1,)),
            dma((1,)),
            dma((1,)),
            dma((NY - 1, pieces)),
            dma((NY - 1, pieces)),
            dma((pieces,)),
            dma((pieces,)),
            dma((NY - 1, pieces)),
            dma((NY - 1, pieces)),
        ],
        compiler_params=pltpu.CompilerParams(
            collective_id=0, has_side_effects=True, vmem_limit_bytes=60 << 20
        ),
    )(block_list, block_count, query_key, selection, shrinkage, keys, vals)
    return pl.pallas_call(
        hand_over,
        out_shape=jax.ShapeDtypeStruct((1, pixels, cv), bf),
        in_specs=[hbm],
        out_specs=hbm,
        scratch_shapes=[pltpu.VMEM((1, pixels, cv), bf), dma((N_COPIES,)), dma((N_COPIES,))],
    )(out.reshape(1, pixels, cv))


def solution(mesh):
    in_specs = (
        P(None, "space", None),
        P(None, "space", None),
        P("tm", "space", None),
        P("tm", "space"),
        P("tm", "space", None),
        P("space", None),
        P("space"),
    )
    out_specs = P(None, "space", None)
    return jax.shard_map(
        functools.partial(shards, mesh.shape["space"]),
        mesh=mesh,
        in_specs=in_specs,
        out_specs=out_specs,
        check_vma=False,
    )
```
